128 devices in a mesh: depth: 8 (over z, x_hi), dp: 16 (over y, x_lo, core).
Axes of the slice: x: 4 (x_hi: 2, x_lo: 2; x = x_hi * 2 + x_lo), y: 4, z: 4, core: 2. Of those that a mesh axis runs over, the one named last changes fastest.
Arguments:
- layer_inputs: float32 [8, 6144, 2048], P('depth', 'dp'), may hold values from -6 to 6
- weights: float32 [8, 2048, 2048], P('depth', 'dp'), may hold values from -6 to 6
- offsets: float32 [8, 2048], P('depth', 'dp'), may hold values from -3 to 3
- layer_outputs: float32 [8, 6144, 2048], P('depth', 'dp'), may hold values from 0 to 2
- multipliers: float32 [8, 6144, 2048], P('depth', 'dp'), may hold values from -3 to 3
Outputs:
- new_inputs: float32 [8, 6144, 2048], P('depth', 'dp')
- new_weights: float32 [8, 2048, 2048], P('depth', 'dp')
- new_offsets: float32 [8, 2048], P('depth', 'dp')
- new_outputs: float32 [8, 6144, 2048], P('depth', 'dp')
- new_multipliers: float32 [8, 6144, 2048], P('depth', 'dp')
The draws below stay inside these ranges and needn't reach their ends.
All inputs are finite; a program needn't handle non-finite values.
Results may differ from the reference program's by a relative error of at most 0.00008.
Values sent between devices are 32-bit elements; how exact they have to be, the bound alone decides.
No kernel may reach another device: no remote copies, remote signals or barrier semaphores. Data moves between devices by JAX's collectives and lax.ppermute only.
A program may use at most 128 MiB of HBM per device.

```python
import math
import jax
import jax.numpy as jnp
from jax import lax

D = 2048
LAYERS = 8
SAMPLES = 6144


def block_scale(key, extent, pieces, smallest, high):
    level = 1.0
    for position, parts in pieces:
        draws = jax.random.uniform(jax.random.fold_in(jax.random.fold_in(key, 6), position), (parts,), jnp.float32, smallest / len(pieces), high / len(pieces))
        level = level * jnp.repeat(jnp.exp(draws), extent[position] // parts).reshape((-1,) + (1,) * (len(extent) - 1 - position))
    return level


def centred(key, shape, spread, most, shards=(), held_as=jnp.bfloat16):
    result = jax.random.normal(key, shape, jnp.float32) * spread
    if len(shards) > 0:
        result = block_scale(key, shape, shards, -0.22, 0.18) * result
    return jnp.clip(result, min=-most, max=most).astype(held_as)


def setup_inputs(seed: int = 0) -> dict:
    streams_of = jax.random.split(jax.random.key(seed), 6)
    return {
        "layer_inputs": centred(streams_of[0], (LAYERS, SAMPLES, D), 1.0, 6.0, ((0, 8), (1, 16)), jnp.float32),
        "weights": centred(streams_of[1], (LAYERS, D, D), 1.0, 6.0, ((0, 8), (1, 16)), jnp.float32),
        "offsets": centred(streams_of[2], (LAYERS, D), 0.5, 3.0, ((0, 8), (1, 16)), jnp.float32),
        "layer_outputs": jnp.clip(2.0 * jax.random.uniform(streams_of[3], (LAYERS, SAMPLES, D), jnp.float32) ** block_scale(streams_of[3], (LAYERS, SAMPLES, D), ((0, 8), (1, 16)), -0.2, 0.2), 0.0, 2.0),
        "multipliers": centred(streams_of[4], (LAYERS, SAMPLES, D), 0.5, 3.0, ((0, 8), (1, 16)), jnp.float32),
    }


fit_weight = 1.0
penalty = 1.0
step_input = 0.5

def reference(layer_inputs, weights, offsets, layer_outputs, multipliers):
    highest = lax.Precision.HIGHEST
    scaling = 1.0 / math.sqrt(D)
    samples = layer_inputs.shape[1]
    step_weight = 8.0 / math.sqrt(samples)
    step_offset = 0.5 / math.sqrt(samples)
    affine = scaling * jnp.einsum('lsd,lkd->lsk', layer_inputs, weights, precision=highest) + offsets[:, None, :]
    misfit = affine - layer_outputs
    pulled = scaling * jnp.einsum('lsk,lkd->lsd', misfit, weights, precision=highest)
    zero_layer = jnp.zeros_like(layer_inputs[:1])
    prev_outputs = jnp.concatenate([zero_layer, layer_outputs[:-1]], axis=0)
    prev_multipliers = jnp.concatenate([zero_layer, multipliers[:-1]], axis=0)
    gradient = fit_weight * pulled + prev_multipliers + penalty * (layer_inputs - prev_outputs)
    stepped = layer_inputs - step_input * gradient
    layer_ids = jnp.arange(layer_inputs.shape[0])[:, None, None]
    new_inputs = jnp.where(layer_ids == 0, layer_inputs, stepped)
    weight_grad = fit_weight * scaling * jnp.einsum('lsk,lsd->lkd', misfit, layer_inputs, precision=highest)
    new_weights = weights - step_weight * weight_grad
    new_offsets = offsets - step_offset * fit_weight * lax.optimization_barrier(jnp.sum(misfit, axis=1))
    next_inputs = jnp.concatenate([new_inputs[1:], zero_layer], axis=0)
    is_last = layer_ids == layer_inputs.shape[0] - 1
    coupled = jnp.maximum(0.0, (fit_weight * affine + penalty * next_inputs + multipliers) / (fit_weight + penalty))
    new_outputs = jnp.where(is_last, jnp.maximum(0.0, affine), coupled)
    new_multipliers = jnp.where(is_last, multipliers, multipliers + penalty * (next_inputs - new_outputs))
    return (new_inputs, new_weights, new_offsets, new_outputs, new_multipliers)
```

```python
import functools
import math

import jax
import jax.numpy as jnp
from jax import lax
from jax.experimental import pallas as pl
from jax.experimental.pallas import tpu as pltpu
from jax.sharding import PartitionSpec as P

D = 2048
BLOCK = 128
PAIR = 2 * BLOCK
QUAD = 4 * BLOCK
TAU_P = 0.5
TILES = 2
WIDE = 512
SMALL = pl.CostEstimate(flops=1024, bytes_accessed=1024, transcendentals=0)


def dp_move(v, step):
    return lax.ppermute(v, "dp", [(i, step(i)) for i in range(16)])


def core_swap(v):
    return dp_move(v, lambda i: i ^ 1)


def x_swap(v):
    return dp_move(v, lambda i: i ^ 2)


def y_shift(v, k):
    return dp_move(v, lambda i: (i + 4 * k) % 16)


def depth_shift(v, k):
    n = lax.axis_size("depth")
    return lax.ppermute(v, "depth", [(i, i + k) for i in range(n) if 0 <= i + k < n])


def after(v, *deps):
    return lax.optimization_barrier((v, *deps))[0]


def parity_kernel(s_ref, x_ref, mine_ref, theirs_ref):
    first_x, even = s_ref[1] == 0, s_ref[2] == 0
    tiles = [x_ref[:, n * BLOCK : (n + 1) * BLOCK] for n in range(4)]
    for pos in range(2):
        cols = slice(pos * BLOCK, (pos + 1) * BLOCK)
        a = jnp.where(first_x, tiles[2 * pos], tiles[2 - 2 * pos])
        b = jnp.where(first_x, tiles[2 * pos + 1], tiles[3 - 2 * pos])
        mine_ref[:, cols] = jnp.where(even, a, b)
        theirs_ref[:, cols] = jnp.where(even, b, a)


def split_parity(place, v):
    rows = v.shape[0]
    half = jax.ShapeDtypeStruct((4, rows, PAIR), v.dtype)
    return pl.pallas_call(
        parity_kernel,
        out_shape=(half, half),
        grid_spec=pltpu.PrefetchScalarGridSpec(
            num_scalar_prefetch=1,
            grid=(4,),
            in_specs=[pl.BlockSpec((rows, QUAD), lambda k, s: (0, lax.rem(s[0] + k, 4)))],
            out_specs=[pl.BlockSpec((None, rows, PAIR), lambda k, s: (k, 0, 0))] * 2,
        ),
        cost_estimate=SMALL,
        name="parity",
    )(place, v)


def last_kernel(s_ref, mine_ref, theirs_ref, r_ref, q_ref, u_ref, qo_ref, uo_ref):
    first_x, even, is_last = s_ref[1] == 0, s_ref[2] == 0, s_ref[3] == 1
    mine = [mine_ref[:, :BLOCK], mine_ref[:, BLOCK:]]
    theirs = [theirs_ref[:, :BLOCK], theirs_ref[:, BLOCK:]]
    for xx in range(2):
        a = jnp.where(first_x, mine[xx], mine[1 - xx])
        b = jnp.where(first_x, theirs[xx], theirs[1 - xx])
        for cc, affine in enumerate((jnp.where(even, a, b), jnp.where(even, b, a))):
            n = 2 * xx + cc
            cols = slice(n * BLOCK, (n + 1) * BLOCK)
            q, u = q_ref[:, cols], u_ref[:, cols]
            nxt = r_ref[:, cols] - TAU_P * (u - q)
            coupled = jnp.maximum(0.0, (affine + nxt + u) * 0.5)
            q_new = jnp.where(is_last, jnp.maximum(0.0, affine), coupled)
            qo_ref[:, cols] = q_new
            uo_ref[:, cols] = jnp.where(is_last, u, u + (nxt - q_new))


def last_step(part, parts, place, mine, theirs, r, q, u, so_far):
    rows = q.shape[0] // parts
    half = pl.BlockSpec((None, rows, PAIR), lambda g, s: (lax.rem(g + 4 - s[0], 4), part, 0))
    full = pl.BlockSpec((rows, QUAD), lambda g, s: (part, g))
    out = jax.ShapeDtypeStruct(q.shape, jnp.float32)
    left = pl.BlockSpec(memory_space=pl.ANY)
    kernel = last_kernel if so_far is None else lambda *refs: last_kernel(*refs[:6], *refs[8:])
    more = () if so_far is None else so_far
    return pl.pallas_call(
        kernel,
        out_shape=(out, out),
        grid_spec=pltpu.PrefetchScalarGridSpec(
            num_scalar_prefetch=1,
            grid=(4,),
            in_specs=[half, half, pl.BlockSpec((rows, QUAD), lambda g, s: (0, g)), full, full]
            + [left] * len(more),
            out_specs=[full, full],
        ),
        input_output_aliases={6 + n: n for n in range(len(more))},
        cost_estimate=SMALL,
        name="last_step",
    )(place, mine, theirs, r, q, u, *more)


def dot(a, b, left, right):
    return lax.dot_general(a, b, (((left,), (right,)), ((), ())), preferred_element_type=jnp.float32)


def split(v):
    hi = v.astype(jnp.bfloat16)
    return hi, (v - hi.astype(jnp.float32)).astype(jnp.bfloat16)


def step_kernel(blocks, n_bias, first, apart, ph_ref, pl_ref, *refs):
    n = len(blocks)
    w_refs, q_refs, b_refs = refs[:n], refs[n : 2 * n], refs[2 * n : 2 * n + n_bias]
    refs = refs[2 * n + n_bias :]
    if not first:
        old_ref, refs = refs[0], refs[1:]
    outs, refs = refs[: 1 + apart], refs[1 + apart :]
    aff_ref, refs = refs[0], refs[1:]
    g_refs, (wh, wl, sum_ref) = refs[:n], refs[n:]
    scaling = 1.0 / math.sqrt(D)
    r = pl.program_id(0)

    @pl.when(r == 0)
    def _():
        for j, w_ref in enumerate(w_refs):
            at = slice(j * BLOCK, (j + 1) * BLOCK)
            wh[at, :], wl[at, :] = split(w_ref[...])
        for g_ref in g_refs:
            g_ref[...] = jnp.zeros_like(g_ref)
        sum_ref[...] = jnp.zeros_like(sum_ref)

    ph, plo = ph_ref[...], pl_ref[...]
    product = dot(ph, wh[...], 1, 1) + (dot(ph, wl[...], 1, 1) + dot(plo, wh[...], 1, 1))
    shift = jnp.concatenate([b_refs[a][row : row + 1, :] for a, row in blocks], axis=1)
    affine = scaling * product + shift
    aff_ref[...] = affine
    misfit = affine - jnp.concatenate([q_ref[...] for q_ref in q_refs], axis=1)
    sum_ref[...] += jnp.sum(misfit, axis=0, keepdims=True)
    mh, ml = split(misfit)

    def chunk(step, _):
        cols = pl.ds(pl.multiple_of(step * WIDE, WIDE), WIDE)
        back = dot(mh, wh[:, cols], 1, 0) + (dot(mh, wl[:, cols], 1, 0) + dot(ml, wh[:, cols], 1, 0))
        if not first:
            back += old_ref[:, cols]
        for k, out_ref in enumerate(outs):
            if apart:

                @pl.when(r == k)
                def _():
                    out_ref[:, cols] = back
            else:
                out_ref[:, cols] = back
        grad = dot(mh, ph_ref[:, cols], 0, 0) + (dot(mh, pl_ref[:, cols], 0, 0) + dot(ml, ph_ref[:, cols], 0, 0))
        for j, g_ref in enumerate(g_refs):
            g_ref[:BLOCK, cols] += grad[j * BLOCK : (j + 1) * BLOCK]

    lax.fori_loop(0, D // WIDE, chunk, None)

    @pl.when(r == TILES - 1)
    def _():
        for j, g_ref in enumerate(g_refs):
            g_ref[BLOCK : BLOCK + 1, :BLOCK] = sum_ref[:, j * BLOCK : (j + 1) * BLOCK]


def layer_step(blocks, ph, plo, qs, biases, old, apart=False):
    rows = ph.shape[0]
    tile, n = rows // TILES, len(blocks)
    first = old is None
    by_tile = pl.BlockSpec((tile, D), lambda r: (r, 0))
    fixed = lambda *shape: pl.BlockSpec(shape, lambda r: (0, 0))
    weight_blocks = [w for w, _, _ in blocks]
    targets = [
        pl.BlockSpec((None, tile, BLOCK), functools.partial(lambda k, pos, r: (k, r, pos), *at))
        for _, _, at in blocks
    ]
    args = [ph, plo, *weight_blocks, *[qs] * n, *biases]
    specs = [by_tile, by_tile, *[fixed(BLOCK, D)] * n, *targets, *[fixed(2, BLOCK)] * len(biases)]
    aliases = {}
    if not first:
        args.append(old)
        specs.append(by_tile)
        if not apart:
            aliases = {len(args) - 1: 0}
    f32 = lambda *shape: jax.ShapeDtypeStruct(shape, jnp.float32)
    kernel = functools.partial(step_kernel, [b for _, b, _ in blocks], len(biases), first, apart)
    pulled_shapes = [f32(tile, D)] * 2 if apart else [f32(rows, D)]
    pulled_specs = [fixed(tile, D)] * 2 if apart else [by_tile]
    out = pl.pallas_call(
        kernel,
        grid=(TILES,),
        out_shape=(*pulled_shapes, f32(rows, n * BLOCK), *[f32(BLOCK + 8, D)] * n),
        in_specs=specs,
        out_specs=(
            *pulled_specs,
            pl.BlockSpec((tile, n * BLOCK), lambda r: (r, 0)),
            *[fixed(BLOCK + 8, D)] * n,
        ),
        scratch_shapes=[
            pltpu.VMEM((n * BLOCK, D), jnp.bfloat16),
            pltpu.VMEM((n * BLOCK, D), jnp.bfloat16),
            pltpu.VMEM((1, n * BLOCK), jnp.float32),
        ],
        input_output_aliases=aliases,
        compiler_params=pltpu.CompilerParams(vmem_limit_bytes=58 << 20),
        cost_estimate=SMALL,
        name="layer_step",
    )(*args)
    k = len(pulled_shapes)
    return (out[:k] if apart else out[0]), out[k], out[k + 1 :]


def body(layer_inputs, weights, offsets, layer_outputs, multipliers):
    scaling = 1.0 / math.sqrt(D)
    p, q, u, w = layer_inputs[0], layer_outputs[0], multipliers[0], weights[0]
    rows = p.shape[0]
    samples = rows * lax.axis_size("dp")
    step_weight = 8.0 / math.sqrt(samples)
    step_offset = 0.5 / math.sqrt(samples)
    layer = lax.axis_index("depth")
    last = lax.axis_size("depth") - 1
    me = lax.axis_index("dp")
    y, x, core = me // 4, (me // 2) % 2, me % 2
    place = jnp.stack([y, x, core, layer == last]).astype(jnp.int32)

    hold = lax.optimization_barrier
    third = rows // 3
    thirds = [slice(n * third, (n + 1) * third) for n in range(3)]

    w_x = x_swap(w)
    w_up, w_down = y_shift(w, 1), y_shift(w, -1)
    p_other = core_swap(p)
    q_mine, q_theirs = split_parity(place, q)
    q_other = core_swap(q_theirs)
    b_pair = jnp.concatenate([offsets, x_swap(offsets)], axis=0)
    ahead = [u[t] - q[t] for t in thirds]
    w_x, w_up, w_down, p_other, q_other, q_mine, b_pair, ahead = hold(
        (w_x, w_up, w_down, p_other, q_other, q_mine, b_pair, ahead)
    )
    w_far, wx_down = y_shift(w_up, 1), y_shift(w_x, -1)
    s0 = depth_shift(ahead[0], 1)
    b_up, b_down, b_far = (y_shift(b_pair, k) for k in (1, -1, 2))
    both = jnp.concatenate([p, p_other], axis=0)
    p_top = lax.reduce_precision(both, exponent_bits=8, mantissa_bits=7)
    ph, plo = p_top.astype(jnp.bfloat16), (both - p_top).astype(jnp.bfloat16)
    qs = jnp.concatenate([q_mine, q_other], axis=1)
    blocks = [(w, (0, 0), (0, 0)), (w_x, (0, 1), (0, 1))]
    pulled, a_own, (g_own, g_own_x) = layer_step(blocks, ph, plo, qs, [b_pair], None)
    w_far, wx_down, s0, b_up, b_down, b_far, ph, plo, qs, pulled, a_own, g_own, g_own_x = hold(
        (w_far, wx_down, s0, b_up, b_down, b_far, ph, plo, qs, pulled, a_own, g_own, g_own_x)
    )
    wx_up, wx_far = y_shift(w_x, 1), y_shift(wx_down, -1)
    s1 = depth_shift(after(ahead[1], s0), 1)
    blocks = [
        (w_up, (0, 0), (3, 0)),
        (w_down, (1, 0), (1, 0)),
        (w_far, (2, 0), (2, 0)),
        (wx_down, (1, 1), (1, 1)),
    ]
    biases = [b_up, b_down, b_far]
    pulled, a_some, (g_lo, g_hi, g_far, g_hi_x) = layer_step(blocks, ph, plo, qs, biases, pulled)
    wx_up, wx_far, s1, a_some, pulled, g_lo, g_hi, g_far, g_hi_x = hold(
        (wx_up, wx_far, s1, a_some, pulled, g_lo, g_hi, g_far, g_hi_x)
    )
    far_below, down = y_shift(g_far, 1), y_shift(g_lo, -1)
    s2 = depth_shift(after(ahead[2], s1), 1)
    blocks = [(wx_up, (0, 1), (3, 1)), (wx_far, (1, 1), (2, 1))]
    (ours, theirs), a_rest, (g_lo_x, g_far_x) = layer_step(
        blocks, ph, plo, qs, [b_up, b_far], pulled, apart=True
    )
    pulled_other = core_swap(theirs)
    r = [p[t] - TAU_P * (scaling * (ours[t] + pulled_other[t]) + p[t]) for t in thirds]
    far_below, down, s2, g_lo_x, g_far_x, r, a_rest = hold((far_below, down, s2, g_lo_x, g_far_x, r, a_rest))
    up_x, far_above = y_shift(g_hi_x, 1), y_shift(g_far_x, -1)
    r0 = depth_shift(r[0], -1)
    columns = [
        (a_own[:, :BLOCK], a_own[:, BLOCK:]),
        (a_some[:, BLOCK : 2 * BLOCK], a_some[:, 3 * BLOCK :]),
        (a_some[:, 2 * BLOCK : 3 * BLOCK], a_rest[:, BLOCK:]),
        (a_some[:, :BLOCK], a_rest[:, :BLOCK]),
    ]
    affine = jnp.stack([jnp.concatenate(pair, axis=1) for pair in columns])
    affine_other = core_swap(affine[:, rows:])
    hi_sum = g_hi + far_below
    own_sum = g_own + down
    moved = jnp.concatenate([a - TAU_P * b for a, b in zip(r, (s0, s1, s2))], axis=0)
    inputs_new = jnp.where(layer == 0, p, moved)
    up_x, far_above, r0, affine_mine, affine_other, hi_sum, own_sum, inputs_new, r = hold(
        (up_x, far_above, r0, affine[:, :rows], affine_other, hi_sum, own_sum, inputs_new, r)
    )
    up, down_x = y_shift(hi_sum, 1), y_shift(g_lo_x + far_above, -1)
    r1 = depth_shift(r[1], -1)
    args = (place, affine_mine, affine_other)
    out = last_step(0, 3, *args, r0, q, u, None)
    x_sum = g_own_x + up_x
    up, down_x, r1, out, x_sum, r = hold((up, down_x, r1, out, x_sum, r))
    from_x = x_swap(x_sum + down_x)
    r2 = depth_shift(r[2], -1)
    out = last_step(1, 3, *args, r1, q, u, out)
    own_sum = own_sum + up
    from_x, r2, out, own_sum = hold((from_x, r2, out, own_sum))
    outputs_new, mults_new = last_step(2, 3, *args, r2, q, u, out)
    grad = own_sum + from_x
    weights_new = w - (step_weight * scaling) * grad[:BLOCK]
    offsets_new = offsets - step_offset * grad[BLOCK : BLOCK + 1, :BLOCK]
    return (inputs_new[None], weights_new[None], offsets_new, outputs_new[None], mults_new[None])


def solution(mesh):
    three, two = P("depth", "dp", None), P("depth", "dp")
    specs = (three, three, two, three, three)
    return jax.shard_map(body, mesh=mesh, in_specs=specs, out_specs=specs, check_vma=False)
```

```python
import functools
import math

import jax
import jax.numpy as jnp
from jax import lax
from jax.experimental import pallas as pl
from jax.experimental.pallas import tpu as pltpu
from jax.sharding import PartitionSpec as P

D = 2048
BLOCK = 128
PAIR = 2 * BLOCK
QUAD = 4 * BLOCK
TAU_P = 0.5
TILES = 2
EARLY_TILES = 4
WIDE = 512
SMALL = pl.CostEstimate(flops=1024, bytes_accessed=1024, transcendentals=0)


def dp_move(v, step):
    return lax.ppermute(v, "dp", [(i, step(i)) for i in range(16)])


def core_swap(v):
    return dp_move(v, lambda i: i ^ 1)


def x_swap(v):
    return dp_move(v, lambda i: i ^ 2)


def y_shift(v, k):
    return dp_move(v, lambda i: (i + 4 * k) % 16)


def depth_shift(v, k):
    n = lax.axis_size("depth")
    return lax.ppermute(v, "depth", [(i, i + k) for i in range(n) if 0 <= i + k < n])


def after(v, *deps):
    return lax.optimization_barrier((v, *deps))[0]


def parity_kernel(s_ref, x_ref, mine_ref, theirs_ref):
    first_x, even = s_ref[1] == 0, s_ref[2] == 0
    tiles = [x_ref[:, n * BLOCK : (n + 1) * BLOCK] for n in range(4)]
    for pos in range(2):
        cols = slice(pos * BLOCK, (pos + 1) * BLOCK)
        a = jnp.where(first_x, tiles[2 * pos], tiles[2 - 2 * pos])
        b = jnp.where(first_x, tiles[2 * pos + 1], tiles[3 - 2 * pos])
        mine_ref[:, cols] = jnp.where(even, a, b)
        theirs_ref[:, cols] = jnp.where(even, b, a)


def split_parity(place, v):
    rows = v.shape[0]
    half = jax.ShapeDtypeStruct((4, rows, PAIR), v.dtype)
    return pl.pallas_call(
        parity_kernel,
        out_shape=(half, half),
        grid_spec=pltpu.PrefetchScalarGridSpec(
            num_scalar_prefetch=1,
            grid=(4,),
            in_specs=[pl.BlockSpec((rows, QUAD), lambda k, s: (0, lax.rem(s[0] + k, 4)))],
            out_specs=[pl.BlockSpec((None, rows, PAIR), lambda k, s: (k, 0, 0))] * 2,
        ),
        cost_estimate=SMALL,
        name="parity",
    )(place, v)


def last_kernel(s_ref, mine_ref, theirs_ref, r_ref, q_ref, u_ref, *refs):
    qo_ref, uo_ref = refs[-2:]
    first_x, even, is_last = s_ref[1] == 0, s_ref[2] == 0, s_ref[3] == 1
    for g in range(4):
        k = lax.rem(g + 4 - s_ref[0], 4)
        mine = [mine_ref[k, :, :BLOCK], mine_ref[k, :, BLOCK:]]
        theirs = [theirs_ref[k, :, :BLOCK], theirs_ref[k, :, BLOCK:]]
        for xx in range(2):
            a = jnp.where(first_x, mine[xx], mine[1 - xx])
            b = jnp.where(first_x, theirs[xx], theirs[1 - xx])
            for cc, affine in enumerate((jnp.where(even, a, b), jnp.where(even, b, a))):
                n = 4 * g + 2 * xx + cc
                cols = slice(n * BLOCK, (n + 1) * BLOCK)
                q, u = q_ref[:, cols], u_ref[:, cols]
                nxt = r_ref[:, cols] - TAU_P * (u - q)
                coupled = jnp.maximum(0.0, (affine + nxt + u) * 0.5)
                q_new = jnp.where(is_last, jnp.maximum(0.0, affine), coupled)
                qo_ref[:, cols] = q_new
                uo_ref[:, cols] = jnp.where(is_last, u, u + (nxt - q_new))


def last_step(where, place, mine, theirs, r, q, u, so_far):
    rows = 64
    base = where.start // rows
    half = pl.BlockSpec((4, rows, PAIR), lambda i, s: (0, base + i, 0))
    full = pl.BlockSpec((rows, D), lambda i, s: (base + i, 0))
    out = jax.ShapeDtypeStruct(q.shape, jnp.float32)
    left = pl.BlockSpec(memory_space=pl.ANY)
    more = () if so_far is None else so_far
    return pl.pallas_call(
        last_kernel,
        out_shape=(out, out),
        grid_spec=pltpu.PrefetchScalarGridSpec(
            num_scalar_prefetch=1,
            grid=((where.stop - where.start) // rows,),
            in_specs=[half, half, pl.BlockSpec((rows, D), lambda i, s: (i, 0)), full, full]
            + [left] * len(more),
            out_specs=[full, full],
        ),
        input_output_aliases={6 + n: n for n in range(len(more))},
        cost_estimate=SMALL,
        name="last_step",
    )(place, mine, theirs, r, q, u, *more)


def dot(a, b, left, right):
    return lax.dot_general(a, b, (((left,), (right,)), ((), ())), preferred_element_type=jnp.float32)


def split(v):
    hi = v.astype(jnp.bfloat16)
    return hi, (v - hi.astype(jnp.float32)).astype(jnp.bfloat16)


def split_weights(w_refs, wh, wl):
    for j, w_ref in enumerate(w_refs):
        at = slice(j * BLOCK, (j + 1) * BLOCK)
        wh[at, :], wl[at, :] = split(w_ref[:BLOCK, :])


def affine_and_misfit(ph_ref, pl_ref, wh, wl, w_refs, q_refs, aff_ref, sum_ref):
    ph, plo = ph_ref[...], pl_ref[...]
    product = dot(ph, wh[...], 1, 1) + (dot(ph, wl[...], 1, 1) + dot(plo, wh[...], 1, 1))
    shift = jnp.concatenate([w_ref[BLOCK : BLOCK + 1, :BLOCK] for w_ref in w_refs], axis=1)
    affine = (1.0 / math.sqrt(D)) * product + shift
    aff_ref[...] = affine
    misfit = affine - jnp.concatenate([q_ref[...] for q_ref in q_refs], axis=1)
    sum_ref[...] += jnp.sum(misfit, axis=0, keepdims=True)
    return split(misfit)


def chunked(work):
    lax.fori_loop(0, D // WIDE, lambda n, _: work(pl.ds(pl.multiple_of(n * WIDE, WIDE), WIDE)), None)


def pulled_part(mh, ml, wh, wl, cols):
    return dot(mh, wh[:, cols], 1, 0) + (dot(mh, wl[:, cols], 1, 0) + dot(ml, wh[:, cols], 1, 0))


def add_gradient(mh, ml, ph_ref, pl_ref, g_refs, cols):
    grad = dot(mh, ph_ref[:, cols], 0, 0) + (dot(mh, pl_ref[:, cols], 0, 0) + dot(ml, ph_ref[:, cols], 0, 0))
    for j, g_ref in enumerate(g_refs):
        g_ref[:BLOCK, cols] += grad[j * BLOCK : (j + 1) * BLOCK]


def put_sums(sums, g_refs):
    for j, g_ref in enumerate(g_refs):
        g_ref[BLOCK : BLOCK + 1, :BLOCK] = sums[:, j * BLOCK : (j + 1) * BLOCK]


def step_kernel(n, first, ph_ref, pl_ref, *refs):
    w_refs, q_refs, refs = refs[:n], refs[n : 2 * n], refs[2 * n :]
    if not first:
        old_ref, refs = refs[0], refs[1:]
    out_ref, aff_ref, *refs = refs
    g_refs, (wh, wl, sum_ref) = refs[:n], refs[n:]
    r = pl.program_id(0)

    @pl.when(r == 0)
    def _():
        split_weights(w_refs, wh, wl)
        for g_ref in g_refs:
            g_ref[...] = jnp.zeros_like(g_ref)
        sum_ref[...] = jnp.zeros_like(sum_ref)

    mh, ml = affine_and_misfit(ph_ref, pl_ref, wh, wl, w_refs, q_refs, aff_ref, sum_ref)

    def work(cols):
        back = pulled_part(mh, ml, wh, wl, cols)
        out_ref[:, cols] = back if first else old_ref[:, cols] + back
        add_gradient(mh, ml, ph_ref, pl_ref, g_refs, cols)

    chunked(work)

    @pl.when(r == TILES - 1)
    def _():
        put_sums(sum_ref[...], g_refs)


def early_kernel(n, ph_ref, pl_ref, *refs):
    w_refs, q_refs, refs = refs[:n], refs[n : 2 * n], refs[2 * n :]
    old_ref, theirs_ref, ours_ref, aff_ref, mh_ref, ml_ref, sum_ref, wh, wl = refs
    r = pl.program_id(0)

    @pl.when(r == 0)
    def _():
        split_weights(w_refs, wh, wl)
        sum_ref[...] = jnp.zeros_like(sum_ref)

    mh, ml = affine_and_misfit(ph_ref, pl_ref, wh, wl, w_refs, q_refs, aff_ref, sum_ref)
    mh_ref[...], ml_ref[...] = mh, ml

    def work(cols):
        back = old_ref[:, cols] + pulled_part(mh, ml, wh, wl, cols)
        for k, out_ref in enumerate((theirs_ref, ours_ref)):

            @pl.when(r // (EARLY_TILES // 2) == k)
            def _():
                out_ref[:, cols] = back

    chunked(work)


def late_kernel(n, ph_ref, pl_ref, mh_ref, ml_ref, sum_ref, *g_refs):
    r = pl.program_id(0)

    @pl.when(r == 0)
    def _():
        for g_ref in g_refs:
            g_ref[...] = jnp.zeros_like(g_ref)

    mh, ml = mh_ref[...], ml_ref[...]
    chunked(lambda cols: add_gradient(mh, ml, ph_ref, pl_ref, g_refs, cols))

    @pl.when(r == TILES - 1)
    def _():
        put_sums(sum_ref[...], g_refs)


def f32(*shape):
    return jax.ShapeDtypeStruct(shape, jnp.float32)


def bf16(*shape):
    return jax.ShapeDtypeStruct(shape, jnp.bfloat16)


def fixed(*shape):
    return pl.BlockSpec(shape, lambda r: (0, 0))


def in_tiles(tiles, kernel, args, in_specs, out_shape, out_specs, scratch, aliases, name):
    return pl.pallas_call(
        kernel,
        grid=(tiles,),
        out_shape=tuple(out_shape),
        in_specs=in_specs,
        out_specs=tuple(out_specs),
        scratch_shapes=scratch,
        input_output_aliases=aliases,
        compiler_params=pltpu.CompilerParams(vmem_limit_bytes=(22 + 6 * len(out_shape)) << 20),
        cost_estimate=SMALL,
        name=name,
    )(*args)


def target_specs(blocks, tile, which):
    return [
        pl.BlockSpec((None, tile, BLOCK), functools.partial(lambda k, pos, r: (k, which(r), pos), *at))
        for _, at in blocks
    ]


def layer_step(blocks, ph, plo, qs, old):
    rows = ph.shape[0]
    tile, n = rows // TILES, len(blocks)
    by_tile = pl.BlockSpec((tile, D), lambda r: (r, 0))
    args = [ph, plo, *[w for w, _ in blocks], *[qs] * n]
    specs = [by_tile, by_tile, *[fixed(BLOCK + 8, D)] * n, *target_specs(blocks, tile, lambda r: r)]
    if old is not None:
        args.append(old)
        specs.append(by_tile)
    out = in_tiles(
        TILES,
        functools.partial(step_kernel, n, old is None),
        args,
        specs,
        [f32(rows, D), f32(rows, n * BLOCK), *[f32(BLOCK + 8, D)] * n],
        [by_tile, pl.BlockSpec((tile, n * BLOCK), lambda r: (r, 0)), *[fixed(BLOCK + 8, D)] * n],
        [
            pltpu.VMEM((n * BLOCK, D), jnp.bfloat16),
            pltpu.VMEM((n * BLOCK, D), jnp.bfloat16),
            pltpu.VMEM((1, n * BLOCK), jnp.float32),
        ],
        {} if old is None else {len(args) - 1: 0},
        "layer_step",
    )
    return out[0], out[1], out[2:]


def early_step(blocks, ph, plo, qs, old):
    rows = ph.shape[0]
    tile, n = rows // EARLY_TILES, len(blocks)
    half = EARLY_TILES // 2
    back = lambda r: lax.rem(r + half, EARLY_TILES)
    other_half = pl.BlockSpec((tile, D), lambda r: (jnp.minimum(r, half - 1), 0))
    own_half = pl.BlockSpec((tile, D), lambda r: (jnp.maximum(r - half, 0), 0))
    by_tile = lambda wide: pl.BlockSpec((tile, wide), lambda r: (back(r), 0))
    args = [ph, plo, *[w for w, _ in blocks], *[qs] * n, old]
    specs = [by_tile(D), by_tile(D), *[fixed(BLOCK + 8, D)] * n, *target_specs(blocks, tile, back)]
    specs.append(by_tile(D))
    wide = n * BLOCK
    return in_tiles(
        EARLY_TILES,
        functools.partial(early_kernel, n),
        args,
        specs,
        [f32(rows // 2, D), f32(rows // 2, D), f32(rows, wide), bf16(rows, wide), bf16(rows, wide), f32(1, wide)],
        [other_half, own_half, *[by_tile(wide)] * 3, fixed(1, wide)],
        [pltpu.VMEM((wide, D), jnp.bfloat16)] * 2,
        {},
        "early_step",
    )


def late_step(n, ph, plo, mh, ml, sums):
    rows = ph.shape[0]
    tile, wide = rows // TILES, n * BLOCK
    by_tile = lambda w: pl.BlockSpec((tile, w), lambda r: (r, 0))
    return in_tiles(
        TILES,
        functools.partial(late_kernel, n),
        [ph, plo, mh, ml, sums],
        [by_tile(D), by_tile(D), by_tile(wide), by_tile(wide), fixed(1, wide)],
        [f32(BLOCK + 8, D)] * n,
        [fixed(BLOCK + 8, D)] * n,
        [],
        {},
        "late_step",
    )


def body(layer_inputs, weights, offsets, layer_outputs, multipliers):
    scaling = 1.0 / math.sqrt(D)
    p, q, u, w = layer_inputs[0], layer_outputs[0], multipliers[0], weights[0]
    rows = p.shape[0]
    samples = rows * lax.axis_size("dp")
    step_weight = 8.0 / math.sqrt(samples)
    step_offset = 0.5 / math.sqrt(samples)
    layer = lax.axis_index("depth")
    last = lax.axis_size("depth") - 1
    me = lax.axis_index("dp")
    y, x, core = me // 4, (me // 2) % 2, me % 2
    place = jnp.stack([y, x, core, layer == last]).astype(jnp.int32)

    hold = lax.optimization_barrier
    parts = [slice(0, 64), slice(64, 320), slice(320, 384)]

    cuts = [slice(0, 136), slice(136, 280), slice(280, 384)]
    bias_rows = jnp.pad(offsets, ((0, 7), (0, D - BLOCK)))
    w = jnp.concatenate([w, bias_rows], axis=0)
    w_x = x_swap(w)
    w_up, w_down = y_shift(w, 1), y_shift(w, -1)
    p_other = core_swap(p)
    q_mine, q_theirs = split_parity(place, after(q, w))
    q_other = core_swap(q_theirs)
    ahead = [u[t] - q[t] for t in cuts]
    w_x, w_up, w_down, p_other, q_mine, q_other, ahead = hold((w_x, w_up, w_down, p_other, q_mine, q_other, ahead))
    both = jnp.concatenate([p, p_other], axis=0)
    p_top = lax.reduce_precision(both, exponent_bits=8, mantissa_bits=7)
    ph, plo = p_top.astype(jnp.bfloat16), (both - p_top).astype(jnp.bfloat16)
    qs = jnp.concatenate([q_mine, q_other], axis=1)
    w_far, wx_down = y_shift(w_up, 1), y_shift(w_x, -1)
    s0 = depth_shift(ahead[0], 1)
    blocks = [(w, (0, 0)), (w_x, (0, 1))]
    pulled, a_own, (g_own, g_own_x) = layer_step(blocks, ph, plo, qs, None)
    w_far, wx_down, s0, ph, plo, qs, pulled, a_own, g_own, g_own_x = hold(
        (w_far, wx_down, s0, ph, plo, qs, pulled, a_own, g_own, g_own_x)
    )
    wx_up, wx_far = y_shift(w_x, 1), y_shift(wx_down, -1)
    s1 = depth_shift(after(ahead[1], s0), 1)
    blocks = [(w_up, (3, 0)), (w_down, (1, 0)), (w_far, (2, 0)), (wx_down, (1, 1))]
    pulled, a_some, (g_lo, g_hi, g_far, g_hi_x) = layer_step(blocks, ph, plo, qs, pulled)
    wx_up, wx_far, s1, a_some, pulled, g_lo, g_hi, g_far, g_hi_x = hold(
        (wx_up, wx_far, s1, a_some, pulled, g_lo, g_hi, g_far, g_hi_x)
    )
    s2 = depth_shift(after(ahead[2], s1), 1)
    up_x, down = y_shift(g_hi_x, 1), y_shift(g_lo, -1)
    blocks = [(wx_up, (3, 1)), (wx_far, (2, 1))]
    theirs, ours, a_rest, mh, ml, sums = early_step(blocks, ph, plo, qs, pulled)
    theirs, ours, a_rest, mh, s2 = hold((theirs, ours, a_rest, mh, s2))
    pulled_other = core_swap(theirs)
    g_lo_x, g_far_x = late_step(2, ph, plo, mh, ml, sums)
    ours, pulled_other, g_lo_x, g_far_x, a_own, a_some, a_rest = hold(
        (ours, pulled_other, g_lo_x, g_far_x, a_own, a_some, a_rest)
    )
    r = [p[t] - TAU_P * (scaling * (ours[t] + pulled_other[t]) + p[t]) for t in parts]
    r0, r1 = depth_shift(r[0], -1), depth_shift(r[1], -1)
    columns = [
        (a_own[:, :BLOCK], a_own[:, BLOCK:]),
        (a_some[:, BLOCK : 2 * BLOCK], a_some[:, 3 * BLOCK :]),
        (a_some[:, 2 * BLOCK : 3 * BLOCK], a_rest[:, BLOCK:]),
        (a_some[:, :BLOCK], a_rest[:, :BLOCK]),
    ]
    affine = jnp.stack([jnp.concatenate(pair, axis=1) for pair in columns])
    some, rest = affine[:3, rows:], affine[3:, rows:]
    affine_other = (core_swap(some), core_swap(after(rest, up_x, down)))
    r0, up_x, down, affine_mine, affine_other, r_tail = hold(
        (r0, up_x, down, affine[:, :rows], affine_other, r[2])
    )
    args = (place, affine_mine, jnp.concatenate(affine_other, axis=0))
    out = last_step(parts[0], *args, r0, q, u, None)
    far_below, far_above = y_shift(after(g_far, r0), 1), y_shift(after(g_far_x, r0), -1)
    up, down_x = y_shift(g_hi + far_below, 1), y_shift(g_lo_x + far_above, -1)
    own_sum = g_own + down
    x_sum = g_own_x + up_x
    r1, out, own_sum, x_sum, up, down_x = hold((r1, out, own_sum, x_sum, up, down_x))
    from_x = x_swap(x_sum + down_x)
    r2 = depth_shift(r_tail, -1)
    out = last_step(parts[1], *args, r1, q, u, out)
    own_sum = own_sum + up
    moved = jnp.concatenate(r, axis=0) - TAU_P * jnp.concatenate([s0, s1, s2], axis=0)
    inputs_new = jnp.where(layer == 0, p, moved)
    scale_weight = step_weight * scaling
    bias = slice(BLOCK, BLOCK + 1)
    weights_new = weights[0] - scale_weight * own_sum[:BLOCK]
    offsets_new = offsets - step_offset * own_sum[bias, :BLOCK]
    weights_new, offsets_new, inputs_new, out, r2 = hold((weights_new, offsets_new, inputs_new, out, r2))
    outputs_new, mults_new = last_step(parts[2], *args, r2, q, u, out)
    weights_new = weights_new - scale_weight * from_x[:BLOCK]
    offsets_new = offsets_new - step_offset * from_x[bias, :BLOCK]
    return (inputs_new[None], weights_new[None], offsets_new, outputs_new[None], mults_new[None])


def solution(mesh):
    three, two = P("depth", "dp", None), P("depth", "dp")
    specs = (three, three, two, three, three)
    return jax.shard_map(body, mesh=mesh, in_specs=specs, out_specs=specs, check_vma=False)
```

```python
import functools
import math

import jax
import jax.numpy as jnp
from jax import lax
from jax.experimental import pallas as pl
from jax.experimental.pallas import tpu as pltpu
from jax.sharding import PartitionSpec as P

D = 2048
BLOCK = 128
PAIR = 2 * BLOCK
QUAD = 4 * BLOCK
TAU_P = 0.5
TILES = 2
EARLY_TILES = 4
WIDE = 512
SMALL = pl.CostEstimate(flops=1024, bytes_accessed=1024, transcendentals=0)


def dp_move(v, step):
    return lax.ppermute(v, "dp", [(i, step(i)) for i in range(16)])


def core_swap(v):
    return dp_move(v, lambda i: i ^ 1)


def x_swap(v):
    return dp_move(v, lambda i: i ^ 2)


def y_shift(v, k):
    return dp_move(v, lambda i: (i + 4 * k) % 16)


def depth_shift(v, k):
    n = lax.axis_size("depth")
    return lax.ppermute(v, "depth", [(i, i + k) for i in range(n) if 0 <= i + k < n])


def after(v, *deps):
    return lax.optimization_barrier((v, *deps))[0]


def parity_kernel(s_ref, x_ref, mine_ref, theirs_ref):
    first_x, even = s_ref[1] == 0, s_ref[2] == 0
    tiles = [x_ref[:, n * BLOCK : (n + 1) * BLOCK] for n in range(4)]
    for pos in range(2):
        cols = slice(pos * BLOCK, (pos + 1) * BLOCK)
        a = jnp.where(first_x, tiles[2 * pos], tiles[2 - 2 * pos])
        b = jnp.where(first_x, tiles[2 * pos + 1], tiles[3 - 2 * pos])
        mine_ref[:, cols] = jnp.where(even, a, b)
        theirs_ref[:, cols] = jnp.where(even, b, a)


def split_parity(place, v):
    rows = v.shape[0]
    half = jax.ShapeDtypeStruct((4, rows, PAIR), v.dtype)
    return pl.pallas_call(
        parity_kernel,
        out_shape=(half, half),
        grid_spec=pltpu.PrefetchScalarGridSpec(
            num_scalar_prefetch=1,
            grid=(4,),
            in_specs=[pl.BlockSpec((rows, QUAD), lambda k, s: (0, lax.rem(s[0] + k, 4)))],
            out_specs=[pl.BlockSpec((None, rows, PAIR), lambda k, s: (k, 0, 0))] * 2,
        ),
        cost_estimate=SMALL,
        name="parity",
    )(place, v)


def last_kernel(s_ref, mine_ref, theirs_ref, r_ref, q_ref, u_ref, *refs):
    qo_ref, uo_ref = refs[-2:]
    first_x, even, is_last = s_ref[1] == 0, s_ref[2] == 0, s_ref[3] == 1
    for g in range(4):
        k = lax.rem(g + 4 - s_ref[0], 4)
        mine = [mine_ref[k, :, :BLOCK], mine_ref[k, :, BLOCK:]]
        theirs = [theirs_ref[k, :, :BLOCK], theirs_ref[k, :, BLOCK:]]
        for xx in range(2):
            a = jnp.where(first_x, mine[xx], mine[1 - xx])
            b = jnp.where(first_x, theirs[xx], theirs[1 - xx])
            for cc, affine in enumerate((jnp.where(even, a, b), jnp.where(even, b, a))):
                n = 4 * g + 2 * xx + cc
                cols = slice(n * BLOCK, (n + 1) * BLOCK)
                q, u = q_ref[:, cols], u_ref[:, cols]
                nxt = r_ref[:, cols] - TAU_P * (u - q)
                coupled = jnp.maximum(0.0, (affine + nxt + u) * 0.5)
                q_new = jnp.where(is_last, jnp.maximum(0.0, affine), coupled)
                qo_ref[:, cols] = q_new
                uo_ref[:, cols] = jnp.where(is_last, u, u + (nxt - q_new))


def last_step(where, place, mine, theirs, r, q, u, so_far):
    rows = 64
    base = where.start // rows
    half = pl.BlockSpec((4, rows, PAIR), lambda i, s: (0, base + i, 0))
    full = pl.BlockSpec((rows, D), lambda i, s: (base + i, 0))
    out = jax.ShapeDtypeStruct(q.shape, jnp.float32)
    left = pl.BlockSpec(memory_space=pl.ANY)
    more = () if so_far is None else so_far
    return pl.pallas_call(
        last_kernel,
        out_shape=(out, out),
        grid_spec=pltpu.PrefetchScalarGridSpec(
            num_scalar_prefetch=1,
            grid=((where.stop - where.start) // rows,),
            in_specs=[half, half, pl.BlockSpec((rows, D), lambda i, s: (i, 0)), full, full]
            + [left] * len(more),
            out_specs=[full, full],
        ),
        input_output_aliases={6 + n: n for n in range(len(more))},
        cost_estimate=SMALL,
        name="last_step",
    )(place, mine, theirs, r, q, u, *more)


def dot(a, b, left, right):
    return lax.dot_general(a, b, (((left,), (right,)), ((), ())), preferred_element_type=jnp.float32)


def split(v):
    hi = v.astype(jnp.bfloat16)
    return hi, (v - hi.astype(jnp.float32)).astype(jnp.bfloat16)


def split_weights(w_refs, wh, wl):
    for j, w_ref in enumerate(w_refs):
        at = slice(j * BLOCK, (j + 1) * BLOCK)
        wh[at, :], wl[at, :] = split(w_ref[:BLOCK, :])


def affine_and_misfit(ph_ref, pl_ref, wh, wl, w_refs, q_refs, aff_ref, sum_ref):
    ph, plo = ph_ref[...], pl_ref[...]
    product = dot(ph, wh[...], 1, 1) + (dot(ph, wl[...], 1, 1) + dot(plo, wh[...], 1, 1))
    shift = jnp.concatenate([w_ref[BLOCK : BLOCK + 1, :BLOCK] for w_ref in w_refs], axis=1)
    affine = (1.0 / math.sqrt(D)) * product + shift
    aff_ref[...] = affine
    misfit = affine - jnp.concatenate([q_ref[...] for q_ref in q_refs], axis=1)
    sum_ref[...] += jnp.sum(misfit, axis=0, keepdims=True)
    return split(misfit)


def chunked(work):
    lax.fori_loop(0, D // WIDE, lambda n, _: work(pl.ds(pl.multiple_of(n * WIDE, WIDE), WIDE)), None)


def pulled_part(mh, ml, wh, wl, cols):
    return dot(mh, wh[:, cols], 1, 0) + (dot(mh, wl[:, cols], 1, 0) + dot(ml, wh[:, cols], 1, 0))


def add_gradient(mh, ml, ph_ref, pl_ref, g_refs, cols):
    grad = dot(mh, ph_ref[:, cols], 0, 0) + (dot(mh, pl_ref[:, cols], 0, 0) + dot(ml, ph_ref[:, cols], 0, 0))
    for j, g_ref in enumerate(g_refs):
        g_ref[:BLOCK, cols] += grad[j * BLOCK : (j + 1) * BLOCK]


def put_sums(sums, g_refs):
    for j, g_ref in enumerate(g_refs):
        g_ref[BLOCK : BLOCK + 1, :BLOCK] = sums[:, j * BLOCK : (j + 1) * BLOCK]


def step_kernel(n, first, ph_ref, pl_ref, *refs):
    w_refs, q_refs, refs = refs[:n], refs[n : 2 * n], refs[2 * n :]
    if not first:
        old_ref, refs = refs[0], refs[1:]
    out_ref, aff_ref, *refs = refs
    g_refs, (wh, wl, sum_ref) = refs[:n], refs[n:]
    r = pl.program_id(0)

    @pl.when(r == 0)
    def _():
        split_weights(w_refs, wh, wl)
        for g_ref in g_refs:
            g_ref[...] = jnp.zeros_like(g_ref)
        sum_ref[...] = jnp.zeros_like(sum_ref)

    mh, ml = affine_and_misfit(ph_ref, pl_ref, wh, wl, w_refs, q_refs, aff_ref, sum_ref)

    def work(cols):
        back = pulled_part(mh, ml, wh, wl, cols)
        out_ref[:, cols] = back if first else old_ref[:, cols] + back
        add_gradient(mh, ml, ph_ref, pl_ref, g_refs, cols)

    chunked(work)

    @pl.when(r == TILES - 1)
    def _():
        put_sums(sum_ref[...], g_refs)


def early_kernel(n, ph_ref, pl_ref, *refs):
    w_refs, q_refs, refs = refs[:n], refs[n : 2 * n], refs[2 * n :]
    old_ref, theirs_ref, ours_ref, aff_ref, mh_ref, ml_ref, sum_ref, wh, wl = refs
    r = pl.program_id(0)

    @pl.when(r == 0)
    def _():
        split_weights(w_refs, wh, wl)
        sum_ref[...] = jnp.zeros_like(sum_ref)

    mh, ml = affine_and_misfit(ph_ref, pl_ref, wh, wl, w_refs, q_refs, aff_ref, sum_ref)
    mh_ref[...], ml_ref[...] = mh, ml

    def work(cols):
        back = old_ref[:, cols] + pulled_part(mh, ml, wh, wl, cols)
        for k, out_ref in enumerate((theirs_ref, ours_ref)):

            @pl.when(r // (EARLY_TILES // 2) == k)
            def _():
                out_ref[:, cols] = back

    chunked(work)


def late_kernel(n, ph_ref, pl_ref, mh_ref, ml_ref, sum_ref, *g_refs):
    r = pl.program_id(0)

    @pl.when(r == 0)
    def _():
        for g_ref in g_refs:
            g_ref[...] = jnp.zeros_like(g_ref)

    mh, ml = mh_ref[...], ml_ref[...]
    chunked(lambda cols: add_gradient(mh, ml, ph_ref, pl_ref, g_refs, cols))

    @pl.when(r == TILES - 1)
    def _():
        put_sums(sum_ref[...], g_refs)


def f32(*shape):
    return jax.ShapeDtypeStruct(shape, jnp.float32)


def bf16(*shape):
    return jax.ShapeDtypeStruct(shape, jnp.bfloat16)


def fixed(*shape):
    return pl.BlockSpec(shape, lambda r: (0, 0))


def in_tiles(tiles, kernel, args, in_specs, out_shape, out_specs, scratch, aliases, name):
    return pl.pallas_call(
        kernel,
        grid=(tiles,),
        out_shape=tuple(out_shape),
        in_specs=in_specs,
        out_specs=tuple(out_specs),
        scratch_shapes=scratch,
        input_output_aliases=aliases,
        compiler_params=pltpu.CompilerParams(vmem_limit_bytes=(22 + 6 * len(out_shape)) << 20),
        cost_estimate=SMALL,
        name=name,
    )(*args)


def target_specs(blocks, tile, which):
    return [
        pl.BlockSpec((None, tile, BLOCK), functools.partial(lambda k, pos, r: (k, which(r), pos), *at))
        for _, at in blocks
    ]


def layer_step(blocks, ph, plo, qs, old):
    rows = ph.shape[0]
    tile, n = rows // TILES, len(blocks)
    by_tile = pl.BlockSpec((tile, D), lambda r: (r, 0))
    args = [ph, plo, *[w for w, _ in blocks], *[qs] * n]
    specs = [by_tile, by_tile, *[fixed(BLOCK + 8, D)] * n, *target_specs(blocks, tile, lambda r: r)]
    if old is not None:
        args.append(old)
        specs.append(by_tile)
    out = in_tiles(
        TILES,
        functools.partial(step_kernel, n, old is None),
        args,
        specs,
        [f32(rows, D), f32(rows, n * BLOCK), *[f32(BLOCK + 8, D)] * n],
        [by_tile, pl.BlockSpec((tile, n * BLOCK), lambda r: (r, 0)), *[fixed(BLOCK + 8, D)] * n],
        [
            pltpu.VMEM((n * BLOCK, D), jnp.bfloat16),
            pltpu.VMEM((n * BLOCK, D), jnp.bfloat16),
            pltpu.VMEM((1, n * BLOCK), jnp.float32),
        ],
        {} if old is None else {len(args) - 1: 0},
        "layer_step",
    )
    return out[0], out[1], out[2:]


def early_step(blocks, ph, plo, qs, old):
    rows = ph.shape[0]
    tile, n = rows // EARLY_TILES, len(blocks)
    half = EARLY_TILES // 2
    back = lambda r: lax.rem(r + half, EARLY_TILES)
    other_half = pl.BlockSpec((tile, D), lambda r: (jnp.minimum(r, half - 1), 0))
    own_half = pl.BlockSpec((tile, D), lambda r: (jnp.maximum(r - half, 0), 0))
    by_tile = lambda wide: pl.BlockSpec((tile, wide), lambda r: (back(r), 0))
    args = [ph, plo, *[w for w, _ in blocks], *[qs] * n, old]
    specs = [by_tile(D), by_tile(D), *[fixed(BLOCK + 8, D)] * n, *target_specs(blocks, tile, back)]
    specs.append(by_tile(D))
    wide = n * BLOCK
    return in_tiles(
        EARLY_TILES,
        functools.partial(early_kernel, n),
        args,
        specs,
        [f32(rows // 2, D), f32(rows // 2, D), f32(rows, wide), bf16(rows, wide), bf16(rows, wide), f32(1, wide)],
        [other_half, own_half, *[by_tile(wide)] * 3, fixed(1, wide)],
        [pltpu.VMEM((wide, D), jnp.bfloat16)] * 2,
        {},
        "early_step",
    )


def late_step(n, ph, plo, mh, ml, sums):
    rows = ph.shape[0]
    tile, wide = rows // TILES, n * BLOCK
    by_tile = lambda w: pl.BlockSpec((tile, w), lambda r: (r, 0))
    return in_tiles(
        TILES,
        functools.partial(late_kernel, n),
        [ph, plo, mh, ml, sums],
        [by_tile(D), by_tile(D), by_tile(wide), by_tile(wide), fixed(1, wide)],
        [f32(BLOCK + 8, D)] * n,
        [fixed(BLOCK + 8, D)] * n,
        [],
        {},
        "late_step",
    )


def body(layer_inputs, weights, offsets, layer_outputs, multipliers):
    scaling = 1.0 / math.sqrt(D)
    p, q, u, w = layer_inputs[0], layer_outputs[0], multipliers[0], weights[0]
    rows = p.shape[0]
    samples = rows * lax.axis_size("dp")
    step_weight = 8.0 / math.sqrt(samples)
    step_offset = 0.5 / math.sqrt(samples)
    layer = lax.axis_index("depth")
    last = lax.axis_size("depth") - 1
    me = lax.axis_index("dp")
    y, x, core = me // 4, (me // 2) % 2, me % 2
    place = jnp.stack([y, x, core, layer == last]).astype(jnp.int32)

    hold = lax.optimization_barrier
    parts = [slice(0, 64), slice(64, 320), slice(320, 384)]

    cuts = [slice(0, 136), slice(136, 280), slice(280, 384)]
    bias_rows = jnp.pad(offsets, ((0, 7), (0, D - BLOCK)))
    w = jnp.concatenate([w, bias_rows], axis=0)
    w_x = x_swap(w)
    w_up, w_down = y_shift(w, 1), y_shift(w, -1)
    p_other = core_swap(p)
    q_mine, q_theirs = split_parity(place, after(q, w))
    q_other = core_swap(q_theirs)
    ahead = [u[t] - q[t] for t in cuts]
    both = jnp.concatenate([p, p_other], axis=0)
    p_top = lax.reduce_precision(both, exponent_bits=8, mantissa_bits=7)
    ph, plo = p_top.astype(jnp.bfloat16), (both - p_top).astype(jnp.bfloat16)
    w_x, w_up, w_down, ph, plo, q_mine, q_other, ahead = hold((w_x, w_up, w_down, ph, plo, q_mine, q_other, ahead))
    qs = jnp.concatenate([q_mine, q_other], axis=1)
    w_far, wx_down = y_shift(w_up, 1), y_shift(w_x, -1)
    s0 = depth_shift(ahead[0], 1)
    blocks = [(w, (0, 0)), (w_x, (0, 1))]
    pulled, a_own, (g_own, g_own_x) = layer_step(blocks, ph, plo, qs, None)
    w_far, wx_down, s0, ph, plo, qs, pulled, a_own, g_own, g_own_x = hold(
        (w_far, wx_down, s0, ph, plo, qs, pulled, a_own, g_own, g_own_x)
    )
    wx_up, wx_far = y_shift(w_x, 1), y_shift(wx_down, -1)
    s1 = depth_shift(after(ahead[1], s0), 1)
    blocks = [(w_up, (3, 0)), (w_down, (1, 0)), (w_far, (2, 0)), (wx_down, (1, 1))]
    pulled, a_some, (g_lo, g_hi, g_far, g_hi_x) = layer_step(blocks, ph, plo, qs, pulled)
    wx_up, wx_far, s1, a_some, pulled, g_lo, g_hi, g_far, g_hi_x = hold(
        (wx_up, wx_far, s1, a_some, pulled, g_lo, g_hi, g_far, g_hi_x)
    )
    s2 = depth_shift(after(ahead[2], s1), 1)
    up_x, down = y_shift(g_hi_x, 1), y_shift(g_lo, -1)
    blocks = [(wx_up, (3, 1)), (wx_far, (2, 1))]
    theirs, ours, a_rest, mh, ml, sums = early_step(blocks, ph, plo, qs, pulled)
    theirs, ours, a_rest, mh, s2 = hold((theirs, ours, a_rest, mh, s2))
    pulled_other = core_swap(theirs)
    g_lo_x, g_far_x = late_step(2, ph, plo, mh, ml, sums)
    ours, pulled_other, g_lo_x, g_far_x, a_own, a_some, a_rest = hold(
        (ours, pulled_other, g_lo_x, g_far_x, a_own, a_some, a_rest)
    )
    r = [p[t] - TAU_P * (scaling * (ours[t] + pulled_other[t]) + p[t]) for t in parts]
    r0, r1 = depth_shift(r[0], -1), depth_shift(r[1], -1)
    columns = [
        (a_own[:, :BLOCK], a_own[:, BLOCK:]),
        (a_some[:, BLOCK : 2 * BLOCK], a_some[:, 3 * BLOCK :]),
        (a_some[:, 2 * BLOCK : 3 * BLOCK], a_rest[:, BLOCK:]),
        (a_some[:, :BLOCK], a_rest[:, :BLOCK]),
    ]
    affine = jnp.stack([jnp.concatenate(pair, axis=1) for pair in columns])
    some, rest = affine[:3, rows:], affine[3:, rows:]
    affine_other = (core_swap(some), core_swap(after(rest, up_x, down)))
    r0, up_x, down, affine_mine, affine_other, r_tail = hold(
        (r0, up_x, down, affine[:, :rows], affine_other, r[2])
    )
    args = (place, affine_mine, jnp.concatenate(affine_other, axis=0))
    out = last_step(parts[0], *args, r0, q, u, None)
    far_below, far_above = y_shift(after(g_far, r0), 1), y_shift(after(g_far_x, r0), -1)
    up, down_x = y_shift(g_hi + far_below, 1), y_shift(g_lo_x + far_above, -1)
    own_sum = g_own + down
    x_sum = g_own_x + up_x
    moved = jnp.concatenate(r, axis=0) - TAU_P * jnp.concatenate([s0, s1, s2], axis=0)
    inputs_new = jnp.where(layer == 0, p, moved)
    r1, out, own_sum, x_sum, up, down_x, inputs_new = hold((r1, out, own_sum, x_sum, up, down_x, inputs_new))
    from_x = x_swap(x_sum + down_x)
    r2 = depth_shift(r_tail, -1)
    out = last_step(parts[1], *args, r1, q, u, out)
    own_sum = own_sum + up
    scale_weight = step_weight * scaling
    bias = slice(BLOCK, BLOCK + 1)
    weights_new = weights[0] - scale_weight * own_sum[:BLOCK]
    offsets_new = offsets - step_offset * own_sum[bias, :BLOCK]
    weights_new, offsets_new, inputs_new, out, r2 = hold((weights_new, offsets_new, inputs_new, out, r2))
    outputs_new, mults_new = last_step(parts[2], *args, r2, q, u, out)
    weights_new = weights_new - scale_weight * from_x[:BLOCK]
    offsets_new = offsets_new - step_offset * from_x[bias, :BLOCK]
    return (inputs_new[None], weights_new[None], offsets_new, outputs_new[None], mults_new[None])


def solution(mesh):
    three, two = P("depth", "dp", None), P("depth", "dp")
    specs = (three, three, two, three, three)
    return jax.shard_map(body, mesh=mesh, in_specs=specs, out_specs=specs, check_vma=False)
```

```python
import functools
import math

import jax
import jax.numpy as jnp
from jax import lax
from jax.experimental import pallas as pl
from jax.experimental.pallas import tpu as pltpu
from jax.sharding import PartitionSpec as P

D = 2048
BLOCK = 128
PAIR = 2 * BLOCK
QUAD = 4 * BLOCK
TAU_P = 0.5
TILES = 2
EARLY_TILES = 2
WIDE = 512
SMALL = pl.CostEstimate(flops=1024, bytes_accessed=1024, transcendentals=0)


def dp_move(v, step):
    return lax.ppermute(v, "dp", [(i, step(i)) for i in range(16)])


def core_swap(v):
    return dp_move(v, lambda i: i ^ 1)


def x_swap(v):
    return dp_move(v, lambda i: i ^ 2)


def y_shift(v, k):
    return dp_move(v, lambda i: (i + 4 * k) % 16)


def depth_shift(v, k):
    n = lax.axis_size("depth")
    return lax.ppermute(v, "depth", [(i, i + k) for i in range(n) if 0 <= i + k < n])


def after(v, *deps):
    return lax.optimization_barrier((v, *deps))[0]


def parity_kernel(s_ref, x_ref, mine_ref, theirs_ref):
    first_x, even = s_ref[1] == 0, s_ref[2] == 0
    tiles = [x_ref[:, n * BLOCK : (n + 1) * BLOCK] for n in range(4)]
    for pos in range(2):
        cols = slice(pos * BLOCK, (pos + 1) * BLOCK)
        a = jnp.where(first_x, tiles[2 * pos], tiles[2 - 2 * pos])
        b = jnp.where(first_x, tiles[2 * pos + 1], tiles[3 - 2 * pos])
        mine_ref[:, cols] = jnp.where(even, a, b)
        theirs_ref[:, cols] = jnp.where(even, b, a)


def split_parity(place, v):
    rows = v.shape[0]
    half = jax.ShapeDtypeStruct((4, rows, PAIR), v.dtype)
    return pl.pallas_call(
        parity_kernel,
        out_shape=(half, half),
        grid_spec=pltpu.PrefetchScalarGridSpec(
            num_scalar_prefetch=1,
            grid=(4,),
            in_specs=[pl.BlockSpec((rows, QUAD), lambda k, s: (0, lax.rem(s[0] + k, 4)))],
            out_specs=[pl.BlockSpec((None, rows, PAIR), lambda k, s: (k, 0, 0))] * 2,
        ),
        cost_estimate=SMALL,
        name="parity",
    )(place, v)


def last_kernel(s_ref, mine_ref, theirs_ref, r_ref, q_ref, u_ref, *refs):
    qo_ref, uo_ref = refs[-2:]
    first_x, even, is_last = s_ref[1] == 0, s_ref[2] == 0, s_ref[3] == 1
    for g in range(4):
        k = lax.rem(g + 4 - s_ref[0], 4)
        mine = [mine_ref[k, :, :BLOCK], mine_ref[k, :, BLOCK:]]
        theirs = [theirs_ref[k, :, :BLOCK], theirs_ref[k, :, BLOCK:]]
        for xx in range(2):
            a = jnp.where(first_x, mine[xx], mine[1 - xx])
            b = jnp.where(first_x, theirs[xx], theirs[1 - xx])
            for cc, affine in enumerate((jnp.where(even, a, b), jnp.where(even, b, a))):
                n = 4 * g + 2 * xx + cc
                cols = slice(n * BLOCK, (n + 1) * BLOCK)
                q, u = q_ref[:, cols], u_ref[:, cols]
                nxt = r_ref[:, cols] - TAU_P * (u - q)
                coupled = jnp.maximum(0.0, (affine + nxt + u) * 0.5)
                q_new = jnp.where(is_last, jnp.maximum(0.0, affine), coupled)
                qo_ref[:, cols] = q_new
                uo_ref[:, cols] = jnp.where(is_last, u, u + (nxt - q_new))


def last_step(where, place, mine, theirs, r, q, u, so_far):
    rows = 64
    base = where.start // rows
    half = pl.BlockSpec((4, rows, PAIR), lambda i, s: (0, base + i, 0))
    full = pl.BlockSpec((rows, D), lambda i, s: (base + i, 0))
    out = jax.ShapeDtypeStruct(q.shape, jnp.float32)
    left = pl.BlockSpec(memory_space=pl.ANY)
    more = () if so_far is None else so_far
    return pl.pallas_call(
        last_kernel,
        out_shape=(out, out),
        grid_spec=pltpu.PrefetchScalarGridSpec(
            num_scalar_prefetch=1,
            grid=((where.stop - where.start) // rows,),
            in_specs=[half, half, pl.BlockSpec((rows, D), lambda i, s: (i, 0)), full, full]
            + [left] * len(more),
            out_specs=[full, full],
        ),
        input_output_aliases={6 + n: n for n in range(len(more))},
        cost_estimate=SMALL,
        name="last_step",
    )(place, mine, theirs, r, q, u, *more)


def dot(a, b, left, right):
    return lax.dot_general(a, b, (((left,), (right,)), ((), ())), preferred_element_type=jnp.float32)


def split(v):
    hi = v.astype(jnp.bfloat16)
    return hi, (v - hi.astype(jnp.float32)).astype(jnp.bfloat16)


def split_weights(w_refs, wh, wl):
    for j, w_ref in enumerate(w_refs):
        at = slice(j * BLOCK, (j + 1) * BLOCK)
        wh[at, :], wl[at, :] = split(w_ref[:BLOCK, :])


def affine_and_misfit(ph_ref, pl_ref, wh, wl, w_refs, q_refs, aff_ref, sum_ref):
    ph, plo = ph_ref[...], pl_ref[...]
    product = dot(ph, wh[...], 1, 1) + (dot(ph, wl[...], 1, 1) + dot(plo, wh[...], 1, 1))
    shift = jnp.concatenate([w_ref[BLOCK : BLOCK + 1, :BLOCK] for w_ref in w_refs], axis=1)
    affine = (1.0 / math.sqrt(D)) * product + shift
    aff_ref[...] = affine
    misfit = affine - jnp.concatenate([q_ref[...] for q_ref in q_refs], axis=1)
    sum_ref[...] += jnp.sum(misfit, axis=0, keepdims=True)
    return split(misfit)


def chunked(work):
    lax.fori_loop(0, D // WIDE, lambda n, _: work(pl.ds(pl.multiple_of(n * WIDE, WIDE), WIDE)), None)


def pulled_part(mh, ml, wh, wl, cols):
    return dot(mh, wh[:, cols], 1, 0) + (dot(mh, wl[:, cols], 1, 0) + dot(ml, wh[:, cols], 1, 0))


def add_gradient(mh, ml, ph_ref, pl_ref, g_refs, cols):
    grad = dot(mh, ph_ref[:, cols], 0, 0) + (dot(mh, pl_ref[:, cols], 0, 0) + dot(ml, ph_ref[:, cols], 0, 0))
    for j, g_ref in enumerate(g_refs):
        g_ref[:BLOCK, cols] += grad[j * BLOCK : (j + 1) * BLOCK]


def put_sums(sums, g_refs):
    for j, g_ref in enumerate(g_refs):
        g_ref[BLOCK : BLOCK + 1, :BLOCK] = sums[:, j * BLOCK : (j + 1) * BLOCK]


def step_kernel(n, first, ph_ref, pl_ref, *refs):
    w_refs, q_refs, refs = refs[:n], refs[n : 2 * n], refs[2 * n :]
    if not first:
        old_ref, refs = refs[0], refs[1:]
    out_ref, aff_ref, *refs = refs
    g_refs, (wh, wl, sum_ref) = refs[:n], refs[n:]
    r = pl.program_id(0)

    @pl.when(r == 0)
    def _():
        split_weights(w_refs, wh, wl)
        for g_ref in g_refs:
            g_ref[...] = jnp.zeros_like(g_ref)
        sum_ref[...] = jnp.zeros_like(sum_ref)

    mh, ml = affine_and_misfit(ph_ref, pl_ref, wh, wl, w_refs, q_refs, aff_ref, sum_ref)

    def work(cols):
        back = pulled_part(mh, ml, wh, wl, cols)
        out_ref[:, cols] = back if first else old_ref[:, cols] + back
        add_gradient(mh, ml, ph_ref, pl_ref, g_refs, cols)

    chunked(work)

    @pl.when(r == TILES - 1)
    def _():
        put_sums(sum_ref[...], g_refs)


def early_kernel(n, ph_ref, pl_ref, *refs):
    w_refs, q_refs, refs = refs[:n], refs[n : 2 * n], refs[2 * n :]
    old_ref, theirs_ref, ours_ref, aff_ref, mh_ref, ml_ref, sum_ref, wh, wl = refs
    r = pl.program_id(0)

    @pl.when(r == 0)
    def _():
        split_weights(w_refs, wh, wl)
        sum_ref[...] = jnp.zeros_like(sum_ref)

    mh, ml = affine_and_misfit(ph_ref, pl_ref, wh, wl, w_refs, q_refs, aff_ref, sum_ref)
    mh_ref[...], ml_ref[...] = mh, ml

    def work(cols):
        back = old_ref[:, cols] + pulled_part(mh, ml, wh, wl, cols)
        for k, out_ref in enumerate((theirs_ref, ours_ref)):

            @pl.when(r // (EARLY_TILES // 2) == k)
            def _():
                out_ref[:, cols] = back

    chunked(work)


def late_kernel(n, ph_ref, pl_ref, mh_ref, ml_ref, sum_ref, *g_refs):
    r = pl.program_id(0)

    @pl.when(r == 0)
    def _():
        for g_ref in g_refs:
            g_ref[...] = jnp.zeros_like(g_ref)

    mh, ml = mh_ref[...], ml_ref[...]
    chunked(lambda cols: add_gradient(mh, ml, ph_ref, pl_ref, g_refs, cols))

    @pl.when(r == TILES - 1)
    def _():
        put_sums(sum_ref[...], g_refs)


def f32(*shape):
    return jax.ShapeDtypeStruct(shape, jnp.float32)


def bf16(*shape):
    return jax.ShapeDtypeStruct(shape, jnp.bfloat16)


def fixed(*shape):
    return pl.BlockSpec(shape, lambda r: (0, 0))


def in_tiles(tiles, kernel, args, in_specs, out_shape, out_specs, scratch, aliases, name):
    return pl.pallas_call(
        kernel,
        grid=(tiles,),
        out_shape=tuple(out_shape),
        in_specs=in_specs,
        out_specs=tuple(out_specs),
        scratch_shapes=scratch,
        input_output_aliases=aliases,
        compiler_params=pltpu.CompilerParams(vmem_limit_bytes=(22 + 6 * len(out_shape)) << 20),
        cost_estimate=SMALL,
        name=name,
    )(*args)


def target_specs(blocks, tile, which):
    return [
        pl.BlockSpec((None, tile, BLOCK), functools.partial(lambda k, pos, r: (k, which(r), pos), *at))
        for _, at in blocks
    ]


def layer_step(blocks, ph, plo, qs, old):
    rows = ph.shape[0]
    tile, n = rows // TILES, len(blocks)
    by_tile = pl.BlockSpec((tile, D), lambda r: (r, 0))
    args = [ph, plo, *[w for w, _ in blocks], *[qs] * n]
    specs = [by_tile, by_tile, *[fixed(BLOCK + 8, D)] * n, *target_specs(blocks, tile, lambda r: r)]
    if old is not None:
        args.append(old)
        specs.append(by_tile)
    out = in_tiles(
        TILES,
        functools.partial(step_kernel, n, old is None),
        args,
        specs,
        [f32(rows, D), f32(rows, n * BLOCK), *[f32(BLOCK + 8, D)] * n],
        [by_tile, pl.BlockSpec((tile, n * BLOCK), lambda r: (r, 0)), *[fixed(BLOCK + 8, D)] * n],
        [
            pltpu.VMEM((n * BLOCK, D), jnp.bfloat16),
            pltpu.VMEM((n * BLOCK, D), jnp.bfloat16),
            pltpu.VMEM((1, n * BLOCK), jnp.float32),
        ],
        {} if old is None else {len(args) - 1: 0},
        "layer_step",
    )
    return out[0], out[1], out[2:]


def early_step(blocks, ph, plo, qs, old):
    rows = ph.shape[0]
    tile, n = rows // EARLY_TILES, len(blocks)
    half = EARLY_TILES // 2
    back = lambda r: lax.rem(r + half, EARLY_TILES)
    other_half = pl.BlockSpec((tile, D), lambda r: (jnp.minimum(r, half - 1), 0))
    own_half = pl.BlockSpec((tile, D), lambda r: (jnp.maximum(r - half, 0), 0))
    by_tile = lambda wide: pl.BlockSpec((tile, wide), lambda r: (back(r), 0))
    args = [ph, plo, *[w for w, _ in blocks], *[qs] * n, old]
    specs = [by_tile(D), by_tile(D), *[fixed(BLOCK + 8, D)] * n, *target_specs(blocks, tile, back)]
    specs.append(by_tile(D))
    wide = n * BLOCK
    return in_tiles(
        EARLY_TILES,
        functools.partial(early_kernel, n),
        args,
        specs,
        [f32(rows // 2, D), f32(rows // 2, D), f32(rows, wide), bf16(rows, wide), bf16(rows, wide), f32(1, wide)],
        [other_half, own_half, *[by_tile(wide)] * 3, fixed(1, wide)],
        [pltpu.VMEM((wide, D), jnp.bfloat16)] * 2,
        {},
        "early_step",
    )


def late_step(n, ph, plo, mh, ml, sums):
    rows = ph.shape[0]
    tile, wide = rows // TILES, n * BLOCK
    by_tile = lambda w: pl.BlockSpec((tile, w), lambda r: (r, 0))
    return in_tiles(
        TILES,
        functools.partial(late_kernel, n),
        [ph, plo, mh, ml, sums],
        [by_tile(D), by_tile(D), by_tile(wide), by_tile(wide), fixed(1, wide)],
        [f32(BLOCK + 8, D)] * n,
        [fixed(BLOCK + 8, D)] * n,
        [],
        {},
        "late_step",
    )


def body(layer_inputs, weights, offsets, layer_outputs, multipliers):
    scaling = 1.0 / math.sqrt(D)
    p, q, u, w = layer_inputs[0], layer_outputs[0], multipliers[0], weights[0]
    rows = p.shape[0]
    samples = rows * lax.axis_size("dp")
    step_weight = 8.0 / math.sqrt(samples)
    step_offset = 0.5 / math.sqrt(samples)
    layer = lax.axis_index("depth")
    last = lax.axis_size("depth") - 1
    me = lax.axis_index("dp")
    y, x, core = me // 4, (me // 2) % 2, me % 2
    place = jnp.stack([y, x, core, layer == last]).astype(jnp.int32)

    hold = lax.optimization_barrier
    parts = [slice(0, 64), slice(64, 320), slice(320, 384)]

    cuts = [slice(0, 112), slice(112, 264), slice(264, 384)]
    bias_rows = jnp.pad(offsets, ((0, 7), (0, D - BLOCK)))
    w = jnp.concatenate([w, bias_rows], axis=0)
    w_x = x_swap(w)
    w_up, w_down = y_shift(w, 1), y_shift(w, -1)
    p_other = core_swap(p)
    q_mine, q_theirs = split_parity(place, after(q, w))
    q_other = core_swap(q_theirs)
    ahead = [u[t] - q[t] for t in cuts]
    both = jnp.concatenate([p, p_other], axis=0)
    p_top = lax.reduce_precision(both, exponent_bits=8, mantissa_bits=7)
    ph, plo = p_top.astype(jnp.bfloat16), (both - p_top).astype(jnp.bfloat16)
    w_x, w_up, w_down, ph, plo, q_mine, q_other, ahead = hold((w_x, w_up, w_down, ph, plo, q_mine, q_other, ahead))
    qs = jnp.concatenate([q_mine, q_other], axis=1)
    w_far, wx_down = y_shift(w_up, 1), y_shift(w_x, -1)
    s0 = depth_shift(ahead[0], 1)
    blocks = [(w, (0, 0)), (w_x, (0, 1))]
    pulled, a_own, (g_own, g_own_x) = layer_step(blocks, ph, plo, qs, None)
    w_far, wx_down, s0, ph, plo, qs, pulled, a_own, g_own, g_own_x = hold(
        (w_far, wx_down, s0, ph, plo, qs, pulled, a_own, g_own, g_own_x)
    )
    wx_up, wx_far = y_shift(w_x, 1), y_shift(wx_down, -1)
    s1 = depth_shift(after(ahead[1], s0), 1)
    blocks = [(w_up, (3, 0)), (w_down, (1, 0)), (w_far, (2, 0)), (wx_down, (1, 1))]
    pulled, a_some, (g_lo, g_hi, g_far, g_hi_x) = layer_step(blocks, ph, plo, qs, pulled)
    wx_up, wx_far, s1, a_some, pulled, g_lo, g_hi, g_far, g_hi_x = hold(
        (wx_up, wx_far, s1, a_some, pulled, g_lo, g_hi, g_far, g_hi_x)
    )
    s2 = depth_shift(after(ahead[2], s1), 1)
    up_x, down = y_shift(g_hi_x, 1), y_shift(g_lo, -1)
    blocks = [(wx_up, (3, 1)), (wx_far, (2, 1))]
    theirs, ours, a_rest, mh, ml, sums = early_step(blocks, ph, plo, qs, pulled)
    theirs, ours, a_rest, mh, s2 = hold((theirs, ours, a_rest, mh, s2))
    pulled_other = core_swap(theirs)
    g_lo_x, g_far_x = late_step(2, ph, plo, mh, ml, sums)
    ours, pulled_other, g_lo_x, g_far_x, a_own, a_some, a_rest = hold(
        (ours, pulled_other, g_lo_x, g_far_x, a_own, a_some, a_rest)
    )
    r = [p[t] - TAU_P * (scaling * (ours[t] + pulled_other[t]) + p[t]) for t in parts]
    r0, r1 = depth_shift(r[0], -1), depth_shift(r[1], -1)
    columns = [
        (a_own[:, :BLOCK], a_own[:, BLOCK:]),
        (a_some[:, BLOCK : 2 * BLOCK], a_some[:, 3 * BLOCK :]),
        (a_some[:, 2 * BLOCK : 3 * BLOCK], a_rest[:, BLOCK:]),
        (a_some[:, :BLOCK], a_rest[:, :BLOCK]),
    ]
    affine = jnp.stack([jnp.concatenate(pair, axis=1) for pair in columns])
    some, rest = affine[:3, rows:], affine[3:, rows:]
    affine_other = (core_swap(some), core_swap(after(rest, up_x, down)))
    r0, up_x, down, affine_mine, affine_other, r_tail = hold(
        (r0, up_x, down, affine[:, :rows], affine_other, r[2])
    )
    args = (place, affine_mine, jnp.concatenate(affine_other, axis=0))
    out = last_step(parts[0], *args, r0, q, u, None)
    far_below, far_above = y_shift(after(g_far, r0), 1), y_shift(after(g_far_x, r0), -1)
    up, down_x = y_shift(g_hi + far_below, 1), y_shift(g_lo_x + far_above, -1)
    own_sum = g_own + down
    x_sum = g_own_x + up_x
    moved = jnp.concatenate(r, axis=0) - TAU_P * jnp.concatenate([s0, s1, s2], axis=0)
    inputs_new = jnp.where(layer == 0, p, moved)
    r1, out, own_sum, x_sum, up, down_x, inputs_new = hold((r1, out, own_sum, x_sum, up, down_x, inputs_new))
    from_x = x_swap(x_sum + down_x)
    r2 = depth_shift(r_tail, -1)
    out = last_step(parts[1], *args, r1, q, u, out)
    own_sum = own_sum + up
    scale_weight = step_weight * scaling
    bias = slice(BLOCK, BLOCK + 1)
    weights_new = weights[0] - scale_weight * own_sum[:BLOCK]
    offsets_new = offsets - step_offset * own_sum[bias, :BLOCK]
    weights_new, offsets_new, inputs_new, out, r2 = hold((weights_new, offsets_new, inputs_new, out, r2))
    outputs_new, mults_new = last_step(parts[2], *args, r2, q, u, out)
    weights_new = weights_new - scale_weight * from_x[:BLOCK]
    offsets_new = offsets_new - step_offset * from_x[bias, :BLOCK]
    return (inputs_new[None], weights_new[None], offsets_new, outputs_new[None], mults_new[None])


def solution(mesh):
    three, two = P("depth", "dp", None), P("depth", "dp")
    specs = (three, three, two, three, three)
    return jax.shard_map(body, mesh=mesh, in_specs=specs, out_specs=specs, check_vma=False)
```
